128 devices in a mesh: orb: 8 (over x, y_lo), grid: 16 (over z, y_hi, core).
Axes of the slice: x: 4, y: 4 (y_hi: 2, y_lo: 2; y = y_hi * 2 + y_lo), z: 4, core: 2. Of those that a mesh axis runs over, the one named last changes fastest.
Arguments:
- coefficients: bfloat16 [32, 32, 32, 2048], P('grid', None, None, 'orb'), may hold values from -6 to 6
- potential: float32 [64, 64, 64], P(None, 'grid'), may hold values from -5 to 5
- rotation: bfloat16 [2048, 2048], P(None, 'orb'), may hold values from -0.125 to 0.125
Outputs:
- hamiltonian: bfloat16 [32, 32, 32, 2048], P('grid', None, None, 'orb')
- rotated: bfloat16 [32, 32, 32, 2048], P('grid', None, None, 'orb')
- projected: float32 [2048, 2048], P('grid', 'orb')
- intersection: float32 [2048, 2048], P('grid', 'orb')
The draws below stay inside these ranges and needn't reach their ends.
All inputs are finite; a program needn't handle non-finite values.
Results may differ from the reference program's by a relative error of at most 0.01.
Values may be sent and summed in bfloat16 or wider, within the bound.
No kernel may reach another device: no remote copies, remote signals or barrier semaphores. Data moves between devices by JAX's collectives and lax.ppermute only.
A program may use at most 64 MiB of HBM per device.

```python
import math
import jax
import jax.numpy as jnp
from jax import lax

KC = 32
NG = 64
ORBITALS = 2048


def spiked(result, stream_key, source, target, parts, factor):
    owner, partner = [(jnp.arange(result.shape[axis_at]) // (result.shape[axis_at] // parts)).reshape([-1 if axis == axis_at else 1 for axis in range(result.ndim)]) for axis_at in (source, target)]
    chosen = jax.random.permutation(stream_key, parts)[partner]
    strong = (owner == chosen) | (owner == (partner + parts // 2) % parts)
    return jnp.where(strong, factor * result, result)


def level_of(rng, shape, cuts, low, high):
    factor_of, own = 1.0, jax.random.fold_in(rng, 6)
    for position, shards_of in cuts:
        draws = jnp.exp(jax.random.uniform(jax.random.fold_in(own, position), (shards_of,), jnp.float32, low / len(cuts), high / len(cuts)))
        factor_of = factor_of * jnp.repeat(draws, shape[position] // shards_of).reshape([-1 if axis == position else 1 for axis in range(len(shape))])
    return factor_of


def scatter_about(rng, shape, deviation, reach, split=(), kind=jnp.bfloat16):
    loudness = level_of(rng, shape, split, -0.22, 0.18) if split else 1.0
    values = jax.random.normal(rng, shape, jnp.float32) * deviation * loudness
    return jnp.minimum(jnp.maximum(values, -reach), reach).astype(kind)


def gaussian_with(stream_key, dims, scale, limit, split, heavy, kind=jnp.bfloat16):
    drawn = scale * jax.random.normal(stream_key, dims, jnp.float32)
    if split:
        drawn = drawn * level_of(stream_key, dims, split, -0.22, 0.18)
    return jnp.clip(spiked(drawn, jax.random.fold_in(stream_key, 3), *heavy), -limit, limit).astype(kind)


def setup_inputs(seed: int = 0) -> dict:
    key_of = jax.random.split(jax.random.key(seed), 4)
    coefficients = gaussian_with(key_of[0], (KC, KC, KC, ORBITALS), 1.0, 6.0, ((0, 16), (3, 8)), (0, 3, 16, 2.0))
    potential = scatter_about(key_of[1], (NG, NG, NG), 1.0, 5.0, ((1, 16),), jnp.float32)
    rotation = scatter_about(key_of[2], (ORBITALS, ORBITALS), ORBITALS ** -0.5, 0.125, ((1, 8),))
    return dict(coefficients=coefficients, potential=potential, rotation=rotation)


def tables():
    grid_points = jnp.arange(NG, dtype=jnp.int32)
    modes = jnp.arange(KC, dtype=jnp.int32) - KC // 2
    phases = grid_points[:, None] * modes[None, :] % NG
    angles = phases.astype(jnp.float32) * (2.0 * math.pi / NG)
    waves = jnp.cos(angles) + jnp.sin(angles)
    forward = (waves / math.sqrt(KC)).astype(jnp.bfloat16)
    backward = (waves.T / math.sqrt(NG)).astype(jnp.bfloat16)
    return (forward, backward)

def kinetic(start_plane, count_planes):
    first_modes = (start_plane + jnp.arange(count_planes, dtype=jnp.int32) - KC // 2).astype(jnp.float32)
    other_modes = (jnp.arange(KC, dtype=jnp.int32) - KC // 2).astype(jnp.float32)
    energy = first_modes[:, None, None] ** 2 + other_modes[None, :, None] ** 2 + other_modes[None, None, :] ** 2
    return 0.5 * energy / float((KC // 2) ** 2)

def apply_whole(orbital_block, potential, forward, backward, energies):
    forward_wide = forward.astype(jnp.float32)
    backward_wide = backward.astype(jnp.float32)
    section_one = jnp.einsum('abkn,zk->abzn', orbital_block.astype(jnp.float32), forward_wide).astype(jnp.bfloat16)
    section_two = jnp.einsum('akzn,yk->ayzn', section_one.astype(jnp.float32), forward_wide).astype(jnp.bfloat16)
    real_space = jnp.einsum('kyzn,xk->xyzn', section_two.astype(jnp.float32), forward_wide)
    weighted = (real_space * potential[:, :, :, None]).astype(jnp.bfloat16)
    back_one = jnp.einsum('xyzn,kx->kyzn', weighted.astype(jnp.float32), backward_wide).astype(jnp.bfloat16)
    back_two = jnp.einsum('ayzn,ky->akzn', back_one.astype(jnp.float32), backward_wide).astype(jnp.bfloat16)
    back_three = jnp.einsum('akzn,jz->akjn', back_two.astype(jnp.float32), backward_wide)
    return (back_three + energies[:, :, :, None] * orbital_block.astype(jnp.float32)).astype(jnp.bfloat16)

def reference(coefficients, potential, rotation):
    forward, backward = tables()
    energies = kinetic(0, KC)
    batch_width = math.gcd(ORBITALS, 64)
    batches = jnp.moveaxis(coefficients.reshape(KC, KC, KC, ORBITALS // batch_width, batch_width), 3, 0)

    def one_batch(orbital_block):
        return apply_whole(orbital_block, potential, forward, backward, energies)
    applied = lax.map(one_batch, batches)
    hamiltonian = jnp.moveaxis(applied, 0, 3).reshape(KC, KC, KC, ORBITALS)
    rows_all = coefficients.reshape(KC * KC * KC, ORBITALS)
    applied_rows = hamiltonian.reshape(KC * KC * KC, ORBITALS)
    rotated = jnp.dot(rows_all, rotation, preferred_element_type=jnp.float32).astype(jnp.bfloat16)
    rotated = rotated.reshape(KC, KC, KC, ORBITALS)
    projected = jnp.dot(rows_all.T, applied_rows, preferred_element_type=jnp.float32) / float(KC * KC * KC)
    intersection = jnp.dot(rows_all.T, rows_all, preferred_element_type=jnp.float32) / float(KC * KC * KC)
    return (hamiltonian, rotated, projected, intersection)
```

```python
import math

import jax
import jax.numpy as jnp
import numpy as np
from jax import lax
from jax.experimental import pallas as pl
from jax.experimental.pallas import tpu as pltpu
from jax.sharding import PartitionSpec as P

KC = 32
NG = 64
F32 = jnp.float32
BF16 = jnp.bfloat16
VM = pltpu.VMEM


def tables():
    points = np.arange(NG)
    modes = np.arange(KC) - KC // 2
    angles = ((points[:, None] * modes[None, :]) % NG).astype(np.float32) * np.float32(
        2.0 * math.pi / NG
    )
    waves = np.cos(angles) + np.sin(angles)
    forward = (waves / np.float32(math.sqrt(KC))).astype(BF16)
    backward = (waves.T / np.float32(math.sqrt(NG))).astype(BF16)
    return forward, backward


def operators():
    forward, backward = tables()
    eye8 = np.eye(8, dtype=np.float32)
    eye4 = np.eye(4, dtype=np.float32)
    fw = forward.astype(np.float32)
    bw = backward.astype(np.float32)
    t1 = np.einsum("xk,ij->xijk", fw, eye8).reshape(512, 256)
    w2 = np.einsum("xk,ij->kijx", fw, eye8).reshape(256, 512)
    t4 = np.einsum("kx,ij->kixj", bw, eye8).reshape(256, 512)
    w5 = np.einsum("kx,ij->kijx", bw, eye8).reshape(256, 512)
    t6 = np.einsum("kx,ij->ixjk", bw, eye4).reshape(256, 128)
    return [jnp.asarray(t.astype(BF16)) for t in (t1, w2, t4, w5, t6)]


def energies():
    modes = (np.arange(KC) - KC // 2).astype(np.float32) ** 2
    first = np.repeat(modes, 8)[:, None] + np.zeros((1, 128), np.float32)
    other = (modes[:, None] + modes[None, :]).reshape(1, KC * KC)
    scale = np.float32(0.5 / (KC // 2) ** 2)
    return jnp.asarray(first * scale), jnp.asarray(other * scale)


def nt(a, b):
    return lax.dot_general(a, b, (((1,), (1,)), ((), ())), preferred_element_type=F32)


def nn(a, b):
    return jnp.dot(a, b, preferred_element_type=F32)


def turn_kernel(c_ref, blocks_ref, rows_ref):
    first = c_ref[0].astype(F32).T
    second = c_ref[1].astype(F32).T
    both = jnp.concatenate([first.reshape(16, 8, 1024), second.reshape(16, 8, 1024)], axis=1)
    blocks_ref[...] = both.astype(BF16).reshape(8, 32, 1024)
    rows_ref[:, :1024] = first.astype(BF16)
    rows_ref[:, 1024:] = second.astype(BF16)


def turn(c3):
    return pl.pallas_call(
        turn_kernel,
        grid=(2,),
        in_specs=[pl.BlockSpec((2, 1024, 128), lambda i: (0, 0, i))],
        out_specs=[
            pl.BlockSpec((8, 32, 1024), lambda i: (i, 0, 0)),
            pl.BlockSpec((128, 2048), lambda i: (i, 0)),
        ],
        out_shape=[
            jax.ShapeDtypeStruct((16, 32, 1024), BF16),
            jax.ShapeDtypeStruct((256, 2048), BF16),
        ],
        name="turn",
    )(c3)


def unturn_kernel(h_ref, out_ref, rows_ref):
    h = h_ref[...].astype(F32).reshape(16, 16, 1024)
    first = h[:, :8].reshape(128, 1024)
    second = h[:, 8:].reshape(128, 1024)
    out_ref[0] = first.T.astype(BF16)
    out_ref[1] = second.T.astype(BF16)
    rows_ref[:, :1024] = first.astype(BF16)
    rows_ref[:, 1024:] = second.astype(BF16)


def unturn(h):
    return pl.pallas_call(
        unturn_kernel,
        grid=(2,),
        in_specs=[pl.BlockSpec((8, 32, 1024), lambda i: (i, 0, 0))],
        out_specs=[
            pl.BlockSpec((2, 1024, 128), lambda i: (0, 0, i)),
            pl.BlockSpec((128, 2048), lambda i: (i, 0)),
        ],
        out_shape=[
            jax.ShapeDtypeStruct((2, 1024, 256), BF16),
            jax.ShapeDtypeStruct((256, 2048), BF16),
        ],
        name="unturn",
    )(h)


def apply_kernel(where_ref, x_ref, v_ref, t1_ref, w2_ref, t4_ref, w5_ref, t6_ref, e1_ref, e2_ref,
                 h_ref, y_ref, u_ref):
    z = where_ref[0]
    x = x_ref[...].reshape(256, 1024)
    parts = [
        nt(t1_ref[...], x[:, 256 * q : 256 * q + 256]).reshape(64, 8, 256) for q in range(4)
    ]
    y_ref[:, :16, :] = jnp.concatenate(parts[:2], axis=1).astype(BF16)
    y_ref[:, 16:, :] = jnp.concatenate(parts[2:], axis=1).astype(BF16)
    low = lax.broadcasted_iota(jnp.int32, (512, 128), 1) < 64
    for p in range(4):
        v = jnp.concatenate(
            [v_ref[lax.rem(b - z + 4, 4), :, p].reshape(128, 128) for b in range(4)], axis=0
        ).astype(F32)
        swapped = pltpu.roll(v, 64, 1)
        tiles = (jnp.where(low, v, swapped), jnp.where(low, swapped, v))
        slabs = []
        for i in range(2):
            y = y_ref[16 * p + 8 * i : 16 * p + 8 * i + 8].reshape(256, 256)
            half = nn(y, w2_ref[...]).astype(BF16)
            real = nn(t1_ref[...], half)
            weighted = jnp.concatenate(
                [real[:, 128 * j : 128 * j + 128] * tiles[i] for j in range(4)], axis=1
            ).astype(BF16)
            slabs.append(nn(t4_ref[...], weighted).reshape(32, 8, 512))
        u_ref[:, 16 * p : 16 * p + 16, :] = jnp.concatenate(slabs, axis=1).astype(BF16)
    for q in range(8):
        u = u_ref[4 * q : 4 * q + 4].reshape(256, 512)
        back = nt(w5_ref[...], u).astype(BF16)
        h = nn(back, t6_ref[...])
        lanes = slice(128 * q, 128 * q + 128)
        energy = e1_ref[...] + e2_ref[:, lanes]
        h = h + energy * x_ref[:, :, lanes].reshape(256, 128).astype(F32)
        h_ref[:, :, lanes] = h.astype(BF16).reshape(16, 16, 128)


def apply(x, v, z):
    ops = operators()
    e1, e2 = energies()
    whole = lambda a: pl.BlockSpec(a.shape, lambda i, s, n=a.ndim: (0,) * n)
    return pl.pallas_call(
        apply_kernel,
        grid_spec=pltpu.PrefetchScalarGridSpec(
            num_scalar_prefetch=1,
            grid=(2,),
            in_specs=[pl.BlockSpec((16, 16, 1024), lambda i, s: (0, i, 0)), whole(v)]
            + [whole(t) for t in ops]
            + [whole(e1), whole(e2)],
            out_specs=pl.BlockSpec((16, 16, 1024), lambda i, s: (0, i, 0)),
            scratch_shapes=[VM((64, 32, 256), BF16), VM((32, 64, 512), BF16)],
        ),
        out_shape=jax.ShapeDtypeStruct((16, 32, 1024), BF16),
        name="apply",
    )(z, x, v, *ops, e1, e2)


ROWS_HALF = 1024


def chunk_specs(chunks, rows):
    steps = ROWS_HALF // rows
    specs = []
    for name, _ in chunks:
        if name == "low":
            specs.append(pl.BlockSpec((rows, 256), lambda i, s: (jnp.minimum(i, steps - 1), 0)))
        elif name == "high":
            specs.append(pl.BlockSpec((rows, 256), lambda i, s: (jnp.maximum(i - steps, 0), 0)))
        else:
            specs.append(pl.BlockSpec((rows, 256), lambda i, s: (i, 0)))
    return specs


def gathered(refs, steps):
    step = pl.program_id(0)
    blocks = [r[...] for r in refs[:6]]
    blocks.append(jnp.where(step < steps, refs[6][...], refs[7][...]))
    blocks.append(jnp.where(step < steps, refs[8][...], refs[9][...]))
    return jnp.concatenate(blocks, axis=1)


def gram_kernel(who_ref, *refs):
    lhs_ref, chunk_refs, out_ref, acc_ref = refs[0], refs[1:11], refs[11], refs[12]
    part = nn(lhs_ref[...], gathered(chunk_refs, 2))

    @pl.when(pl.program_id(0) == 0)
    def _():
        acc_ref[...] = part

    @pl.when(pl.program_id(0) > 0)
    def _():
        acc_ref[...] += part

    @pl.when(pl.program_id(0) == 3)
    def _():
        for d in range(8):
            for half in range(2):
                at = 256 * d + 128 * half
                out_ref[2 * who_ref[d] + half] = acc_ref[:, at : at + 128].astype(BF16)


def gram(lhs, chunks, who):
    return pl.pallas_call(
        gram_kernel,
        grid_spec=pltpu.PrefetchScalarGridSpec(
            num_scalar_prefetch=1,
            grid=(4,),
            in_specs=[pl.BlockSpec((256, 512), lambda i, s: (0, i))] + chunk_specs(chunks, 512),
            out_specs=pl.BlockSpec((16, 256, 128), lambda i, s: (0, 0, 0)),
            scratch_shapes=[VM((256, 2048), F32)],
        ),
        out_shape=jax.ShapeDtypeStruct((16, 256, 128), BF16),
        name="gram",
    )(who, lhs, *[c for _, c in chunks])


def rotate_kernel(who_ref, *refs):
    r_ref, chunk_refs, out_ref, turned = refs[0], refs[1:11], refs[11], refs[12]

    @pl.when(pl.program_id(0) == 0)
    def _():
        for d in range(8):
            at = pl.multiple_of(who_ref[d] * 256, 256)
            turned[256 * d : 256 * d + 256, :] = r_ref[pl.ds(at, 256), :]

    out_ref[...] = nn(gathered(chunk_refs, 4), turned[...]).astype(BF16)


def rotate(r, chunks, who):
    return pl.pallas_call(
        rotate_kernel,
        grid_spec=pltpu.PrefetchScalarGridSpec(
            num_scalar_prefetch=1,
            grid=(8,),
            in_specs=[pl.BlockSpec((2048, 256), lambda i, s: (0, 0))] + chunk_specs(chunks, 256),
            out_specs=pl.BlockSpec((256, 256), lambda i, s: (i, 0)),
            scratch_shapes=[VM((2048, 256), BF16)],
        ),
        out_shape=jax.ShapeDtypeStruct((2048, 256), BF16),
        name="rotate",
    )(who, r, *[c for _, c in chunks])


def along_x(step):
    return [(x * 2 + y, ((x + step) % 4) * 2 + y) for x in range(4) for y in range(2)]


SWAP_Y = [(o, o ^ 1) for o in range(8)]
SWAP_CORE = [(g, g ^ 1) for g in range(16)]
SWAP_FAR = [(g, g ^ 2) for g in range(16)]


def along_z(step):
    return [(g, (g + 4 * step) % 16) for g in range(16)]


def spread_potential(potential, g):
    v = potential.transpose(2, 1, 0).reshape(4, 2, 8, 4, 64)
    v = v.transpose(0, 3, 2, 1, 4).reshape(4, 32, 128).astype(BF16)
    other = lax.ppermute(v, "grid", SWAP_CORE)
    v = jnp.where(g % 2 == 0, jnp.stack([v, other]), jnp.stack([other, v]))
    other = lax.ppermute(v, "grid", SWAP_FAR)
    v = jnp.where(
        (g // 2) % 2 == 0, jnp.concatenate([v, other]), jnp.concatenate([other, v])
    )
    ahead = lax.ppermute(v, "grid", along_z(-1))
    far = lax.ppermute(v, "grid", along_z(2))
    behind = lax.ppermute(v, "grid", along_z(1))
    return jnp.stack([v, ahead, far, behind])


def reduce_rows(partial, g):
    groups = [[2 * i + c for i in range(8)] for c in range(2)]
    pairs = partial.reshape(8, 2, 256, 128)
    core = g % 2
    mine = lax.dynamic_slice_in_dim(pairs, core, 1, 1)[:, 0]
    theirs = lax.dynamic_slice_in_dim(pairs, 1 - core, 1, 1)[:, 0]
    other = lax.ppermute(theirs, "grid", SWAP_CORE)
    total = (mine.astype(F32) + other.astype(F32)).astype(BF16)
    pieces = lax.all_to_all(
        total, "grid", split_axis=0, concat_axis=0, tiled=True, axis_index_groups=groups
    )
    summed = jnp.sum(pieces.astype(F32), axis=0)
    return summed.T * (1.0 / float(KC * KC * KC))


def on_device(coefficients, potential, rotation):
    g = lax.axis_index("grid")
    o = lax.axis_index("orb")
    own = coefficients.reshape(2048, 256)
    behind = lax.ppermute(own, "orb", along_x(1))
    ahead = lax.ppermute(own, "orb", along_x(-1))
    side = lax.ppermute(own, "orb", SWAP_Y)
    blocks, rows = turn(coefficients.reshape(2, 1024, 256))
    spread = lax.all_to_all(blocks, "grid", split_axis=0, concat_axis=0, tiled=True)
    v = spread_potential(potential, g)
    far_low = lax.ppermute(behind[:1024], "orb", along_x(1))
    far_high = lax.ppermute(ahead[1024:], "orb", along_x(-1))
    side_behind = lax.ppermute(side, "orb", along_x(1))
    side_ahead = lax.ppermute(side, "orb", along_x(-1))
    side_far_low = lax.ppermute(far_low, "orb", SWAP_Y)
    side_far_high = lax.ppermute(far_high, "orb", SWAP_Y)
    x, y = o // 2, o % 2
    xs = jnp.stack([x, x + 3, x + 1, x, x + 3, x + 1, x + 2, x + 2]) % 4
    ys = jnp.stack([y, y, y, 1 - y, 1 - y, 1 - y, y, 1 - y])
    who = (xs * 2 + ys).astype(jnp.int32)
    chunks = [
        ("whole", own),
        ("whole", behind),
        ("whole", ahead),
        ("whole", side),
        ("whole", side_behind),
        ("whole", side_ahead),
        ("low", far_low),
        ("high", far_high),
        ("low", side_far_low),
        ("high", side_far_high),
    ]
    applied = apply(spread, v, (g // 4).astype(jnp.int32).reshape(1))
    returned = lax.all_to_all(applied, "grid", split_axis=0, concat_axis=0, tiled=True)
    hamiltonian, applied_rows = unturn(returned)
    intersection = reduce_rows(gram(rows, chunks, who), g)
    projected = reduce_rows(gram(applied_rows, chunks, who), g)
    rotated = rotate(rotation, chunks, who)
    shape = coefficients.shape
    return (hamiltonian.reshape(shape), rotated.reshape(shape), projected, intersection)


def solution(mesh):
    placed = (P("grid", None, None, "orb"), P(None, "grid", None), P(None, "orb"))
    return jax.shard_map(
        on_device,
        mesh=mesh,
        in_specs=placed,
        out_specs=(
            P("grid", None, None, "orb"),
            P("grid", None, None, "orb"),
            P("grid", "orb"),
            P("grid", "orb"),
        ),
        check_vma=False,
    )
```

```python
import functools
import math

import jax
import jax.numpy as jnp
import numpy as np
from jax import lax
from jax.experimental import pallas as pl
from jax.experimental.pallas import tpu as pltpu
from jax.sharding import PartitionSpec as P

KC = 32
NG = 64
F32 = jnp.float32
BF16 = jnp.bfloat16
VM = pltpu.VMEM


def tables():
    points = np.arange(NG)
    modes = np.arange(KC) - KC // 2
    angles = ((points[:, None] * modes[None, :]) % NG).astype(np.float32) * np.float32(
        2.0 * math.pi / NG
    )
    waves = np.cos(angles) + np.sin(angles)
    forward = (waves / np.float32(math.sqrt(KC))).astype(BF16)
    backward = (waves.T / np.float32(math.sqrt(NG))).astype(BF16)
    return forward, backward


def operators():
    forward, backward = tables()
    eye8 = np.eye(8, dtype=np.float32)
    eye4 = np.eye(4, dtype=np.float32)
    fw = forward.astype(np.float32)
    bw = backward.astype(np.float32)
    t1 = np.einsum("xk,ij->xijk", fw, eye8).reshape(512, 256)
    w2 = np.einsum("xk,ij->kijx", fw, eye8).reshape(256, 512)
    t4 = np.einsum("kx,ij->kixj", bw, eye8).reshape(256, 512)
    w5 = np.einsum("kx,ij->kijx", bw, eye8).reshape(256, 512)
    t6 = np.einsum("kx,ij->ixjk", bw, eye4).reshape(256, 128)
    t1 = np.concatenate([t1[:256], t1[256:]], axis=1)
    t6 = np.concatenate([t6.T[:64], t6.T[64:]], axis=1)
    return jnp.asarray(np.concatenate([t1, w2, t4, w5, t6]).astype(BF16))


VMEM_LIMIT = 24 << 20


def pallas(kernel, limit=VMEM_LIMIT, **options):
    params = pltpu.CompilerParams(vmem_limit_bytes=limit)
    return pl.pallas_call(kernel, compiler_params=params, **options)


HBM = pl.BlockSpec(memory_space=pltpu.HBM)
VMEM = pl.BlockSpec(memory_space=VM)
SMEM = pl.BlockSpec(memory_space=pltpu.SMEM)


def nt(a, b):
    return lax.dot_general(a, b, (((1,), (1,)), ((), ())), preferred_element_type=F32)


def nn(a, b):
    return jnp.dot(a, b, preferred_element_type=F32)


def turn_kernel(c_ref, v_ref, blocks_ref, rows_ref, low_ref, high_ref):
    low_ref[...] = c_ref[0]
    high_ref[...] = c_ref[1]
    first = c_ref[0].astype(F32).T
    second = c_ref[1].astype(F32).T
    both = jnp.concatenate([first.reshape(16, 8, 1024), second.reshape(16, 8, 1024)], axis=1)
    blocks_ref[:, :32, :] = both.astype(BF16).reshape(8, 32, 1024)
    columns = [v_ref[:, j, :].T.reshape(4, 2, 8, NG) for j in range(4)]
    tiles = [jnp.concatenate([c[:, 0], c[:, 1]], axis=2) for c in columns]
    for p in range(4):
        for half in range(2):
            lanes = slice(256 * p + 128 * half, 256 * p + 128 * half + 128)
            tile = jnp.concatenate([tiles[2 * half][p], tiles[2 * half + 1][p]], axis=0)
            blocks_ref[:, 32:, lanes] = jnp.broadcast_to(tile.astype(BF16)[None], (8, 16, 128))
    rows_ref[:, :1024] = first.astype(BF16)
    rows_ref[:, 1024:] = second.astype(BF16)


def turn(c3, v):
    return pallas(
        turn_kernel,
        limit=None,
        grid=(2,),
        in_specs=[
            pl.BlockSpec((2, 1024, 128), lambda i: (0, 0, i)),
            pl.BlockSpec((NG, 4, NG), lambda i: (0, 0, 0)),
        ],
        out_specs=[
            pl.BlockSpec((8, 48, 1024), lambda i: (i, 0, 0)),
            pl.BlockSpec((128, 2048), lambda i: (i, 0)),
            pl.BlockSpec((1024, 128), lambda i: (0, i)),
            pl.BlockSpec((1024, 128), lambda i: (0, i)),
        ],
        out_shape=[
            pltpu.HBM((16, 48, 1024), BF16),
            pltpu.HBM((256, 2048), BF16),
            pltpu.HBM((1024, 256), BF16),
            pltpu.HBM((1024, 256), BF16),
        ],
        name="turn",
    )(c3, v)


def orbital_rows(h, plane):
    parts = h.astype(F32).reshape(-1, 16, 1024)[:, 8 * plane : 8 * plane + 8]
    return parts.reshape(-1, 1024)


def unturn_kernel(h_ref, out_ref):
    for plane in range(2):
        out_ref[plane] = orbital_rows(h_ref[...], plane).T.astype(BF16)


def unturn(h):
    return pallas(
        unturn_kernel,
        grid=(2,),
        in_specs=[pl.BlockSpec((8, 32, 1024), lambda i: (i, 0, 0))],
        out_specs=pl.BlockSpec((2, 1024, 128), lambda i: (0, 0, i)),
        out_shape=jax.ShapeDtypeStruct((2, 1024, 256), BF16),
        name="unturn",
    )(h)


def kinetic(lanes_from):
    k1 = lax.broadcasted_iota(jnp.int32, (256, 128), 0) // 8 - KC // 2
    at = lax.broadcasted_iota(jnp.int32, (256, 128), 1) + lanes_from
    k2, k3 = at // KC - KC // 2, at % KC - KC // 2
    return (k1 * k1 + k2 * k2 + k3 * k3).astype(F32) * (0.5 / (KC // 2) ** 2)


def apply_kernel(x_ref, v_ref, tables_ref, h_ref, t1_ref, t6_ref, y_ref, u_ref):
    w2_ref, t4_ref, w5_ref = [tables_ref.at[pl.ds(256 * i, 256)] for i in (1, 2, 3)]
    t1_ref[:256] = tables_ref[:256, :256]
    t1_ref[256:] = tables_ref[:256, 256:]
    t6_ref[:64] = tables_ref[1024:, :256]
    t6_ref[64:] = tables_ref[1024:, 256:]
    for i in range(2):
        parts = [
            nt(t1_ref[...], x_ref[:, :, 256 * q : 256 * q + 256].reshape(256, 256))
            for q in (2 * i, 2 * i + 1)
        ]
        parts = [part.reshape(64, 8, 256) for part in parts]
        y_ref[:, 16 * i : 16 * i + 16, :] = jnp.concatenate(parts, axis=1).astype(BF16)
    low = lax.broadcasted_iota(jnp.int32, (512, 128), 1) < 64
    for p in range(4):
        v = jnp.concatenate(
            [v_ref[:, :, 256 * p + 128 * i : 256 * p + 128 * i + 128] for i in range(2)], axis=1
        )
        v = v.reshape(512, 128).astype(F32)
        swapped = pltpu.roll(v, 64, 1)
        tiles = (jnp.where(low, v, swapped), jnp.where(low, swapped, v))
        slabs = []
        both = nn(y_ref[16 * p : 16 * p + 16].reshape(512, 256), w2_ref[...]).astype(BF16)
        for i in range(2):
            real = nn(t1_ref[...], both[256 * i : 256 * i + 256])
            weighted = jnp.concatenate(
                [real[:, 128 * j : 128 * j + 128] * tiles[i] for j in range(4)], axis=1
            ).astype(BF16)
            slabs.append(nn(t4_ref[...], weighted).reshape(32, 8, 512))
        u_ref[:, 16 * p : 16 * p + 16, :] = jnp.concatenate(slabs, axis=1).astype(BF16)
    for q in range(8):
        u = u_ref[4 * q : 4 * q + 4].reshape(256, 512)
        back = nt(w5_ref[...], u).astype(BF16)
        h = nt(back, t6_ref[...])
        lanes = slice(128 * q, 128 * q + 128)
        h = h + kinetic(128 * q) * x_ref[:, :, lanes].reshape(256, 128).astype(F32)
        h_ref[:, :, lanes] = h.astype(BF16).reshape(16, 16, 128)


def apply(x):
    tables = operators()
    half = pl.BlockSpec((16, 16, 1024), lambda i: (0, i, 0))
    return pallas(
        apply_kernel,
        grid=(2,),
        in_specs=[half, pl.BlockSpec((16, 16, 1024), lambda i: (0, 2, 0))] + [VMEM],
        out_specs=half,
        scratch_shapes=[
            VM((512, 256), BF16),
            VM((128, 256), BF16),
            VM((64, 32, 256), BF16),
            VM((32, 64, 512), BF16),
        ],
        out_shape=pltpu.HBM((16, 32, 1024), BF16),
        name="apply",
    )(x, x, tables)


WHOLE = 3
PIECES = WHOLE + 2 * (8 - WHOLE)
DMA = pltpu.SemaphoreType.DMA


def pieces_of(d):
    if d < WHOLE:
        return [(d, 0, 2048)]
    at = WHOLE + 2 * (d - WHOLE)
    return [(at, 0, 1024), (at + 1, 1024, 1024)]


def used(chunks):
    return [piece for d in chunks for piece, _, _ in pieces_of(d)]


def fetch(refs, buf, sems, chunks):
    at = 0
    for slot, d in enumerate(chunks):
        parts = pieces_of(d)
        for half in range(2):
            if len(parts) == 1:
                source = refs[at].at[pl.ds(1024 * half, 1024)]
            else:
                source = refs[at + half]
            target = buf.at[slot, pl.ds(1024 * half, 1024)]
            pltpu.make_async_copy(source, target, sems.at[slot, half]).start()
        at += len(parts)


def product(lhs, buf, sems, slot):
    for half in range(2):
        target = buf.at[slot, pl.ds(1024 * half, 1024)]
        pltpu.make_async_copy(target, target, sems.at[slot, half]).wait()
    return nn(lhs[...], buf[slot]).astype(BF16)


FIRST = (0, 1, 2)
LATER = (3, 4, 7, 5, 6)


def early_kernel(chunks, rows_ref, *refs):
    chunk_refs, (out_ref, buf, rows, sems, sem) = refs[:-5], refs[-5:]
    load = pltpu.make_async_copy(rows_ref, rows, sem)
    load.start()
    fetch(chunk_refs, buf, sems, chunks)
    load.wait()

    @pl.loop(0, len(chunks))
    def _(slot):
        out_ref[slot] = product(rows, buf, sems, slot)


def early(chunks, rows, pieces):
    operands = [pieces[i] for i in used(chunks)]
    return pallas(
        functools.partial(early_kernel, chunks),
        in_specs=[HBM] * (1 + len(operands)),
        out_specs=VMEM,
        out_shape=pltpu.HBM((len(chunks), 256, 256), BF16),
        scratch_shapes=[
            VM((len(chunks), 2048, 256), BF16),
            VM((256, 2048), BF16),
            DMA((len(chunks), 2)),
            DMA,
        ],
        name="early",
    )(rows, *operands)


def put(where_ref, mine_ref, theirs_ref, d, value):
    block, even = where_ref[3 + d], where_ref[2] == 0
    mine_ref[block] = jnp.where(even, value[:, :128], value[:, 128:])
    theirs_ref[block] = jnp.where(even, value[:, 128:], value[:, :128])


SHARE = jax.ShapeDtypeStruct((8, 256, 128), BF16)


def inter_kernel(where_ref, rows_ref, first_ref, *refs):
    chunk_refs, (mine_ref, theirs_ref, buf, rows, done, sems, loads) = refs[:-7], refs[-7:]
    copies = [
        pltpu.make_async_copy(rows_ref, rows, loads.at[0]),
        pltpu.make_async_copy(first_ref, done, loads.at[1]),
    ]
    copies[0].start()
    fetch(chunk_refs, buf, sems, LATER)
    copies[1].start()
    copies[0].wait()

    @pl.loop(0, len(LATER))
    def _(slot):
        d = jnp.where(slot < 2, slot + 3, jnp.where(slot == 2, 7, slot + 2))
        put(where_ref, mine_ref, theirs_ref, d, product(rows, buf, sems, slot))

    copies[1].wait()
    for slot, d in enumerate(FIRST):
        put(where_ref, mine_ref, theirs_ref, d, done[slot])


def inter(where, rows, first, pieces):
    operands = [pieces[i] for i in used(LATER)]
    return pallas(
        inter_kernel,
        in_specs=[SMEM, HBM, HBM] + [HBM] * len(operands),
        out_specs=[VMEM, VMEM],
        out_shape=[SHARE, SHARE],
        scratch_shapes=[
            VM((len(LATER), 2048, 256), BF16),
            VM((256, 2048), BF16),
            VM((len(FIRST), 256, 256), BF16),
            DMA((len(LATER), 2)),
            DMA((2,)),
        ],
        name="inter",
    )(where, rows, first, *operands)


def proj_kernel(where_ref, h_ref, *refs):
    chunk_refs, (mine_ref, theirs_ref, buf, lhs, sems) = refs[:-5], refs[-5:]
    fetch(chunk_refs, buf, sems, range(8))
    for plane in range(2):
        lanes = slice(1024 * plane, 1024 * plane + 1024)
        lhs[:, lanes] = orbital_rows(h_ref[...], plane).astype(BF16)

    @pl.loop(0, 8)
    def _(d):
        put(where_ref, mine_ref, theirs_ref, d, product(lhs, buf, sems, d))


def proj(where, h, pieces):
    return pallas(
        proj_kernel,
        in_specs=[SMEM, VMEM] + [HBM] * PIECES,
        out_specs=[VMEM, VMEM],
        out_shape=[SHARE, SHARE],
        scratch_shapes=[
            VM((8, 2048, 256), BF16),
            VM((256, 2048), BF16),
            DMA((8, 2)),
        ],
        name="proj",
    )(where, h, *pieces)


BLOCKS4 = jax.ShapeDtypeStruct((4, 256, 128), BF16)
BLOCK = jax.ShapeDtypeStruct((256, 128), BF16)


def total(first, second):
    return (first.astype(F32) + second.astype(F32)).astype(BF16)


def pair_kernel(where_ref, mine_ref, other_ref, keep_ref, give_ref):
    far = where_ref[1]
    for z in range(4):
        keep, give = 2 * z + far, 2 * z + 1 - far
        keep_ref[z] = total(mine_ref[keep], other_ref[keep])
        give_ref[z] = total(mine_ref[give], other_ref[give])


def pair(where, mine, other):
    return pallas(
        pair_kernel,
        in_specs=[SMEM, VMEM, VMEM],
        out_specs=[VMEM, VMEM],
        out_shape=[BLOCKS4, BLOCKS4],
        name="pair",
    )(where, mine, other)


def line_kernel(where_ref, keep_ref, got_ref, *outs):
    for step, out in enumerate(outs):
        z = lax.rem(where_ref[0] + step, 4)
        out[...] = total(keep_ref[z], got_ref[z])


def line(where, keep, got):
    return pallas(
        line_kernel,
        in_specs=[SMEM, VMEM, VMEM],
        out_specs=[VMEM] * 4,
        out_shape=[BLOCK] * 4,
        name="line",
    )(where, keep, got)


def plain_kernel(mine_ref, other_ref, total_ref):
    total_ref[...] = total(mine_ref[...], other_ref[...])


def plain(mine, other):
    block = pl.BlockSpec((4, 256, 128), lambda i: (i, 0, 0))
    return pallas(
        plain_kernel,
        grid=(2,),
        in_specs=[block, block],
        out_specs=block,
        out_shape=pltpu.HBM(SHARE.shape, BF16),
        name="plain",
    )(mine, other)


def finish_kernel(parts_ref, *refs):
    terms, (projected_ref, intersection_ref) = refs[:-2], refs[-2:]
    factor = 1.0 / float(KC * KC * KC)
    summed = parts_ref[0].astype(F32)
    for i in range(1, 8):
        summed = summed + parts_ref[i].astype(F32)
    projected_ref[...] = summed.T * factor
    summed = terms[0][...].astype(F32)
    for term in terms[1:]:
        summed = summed + term[...].astype(F32)
    intersection_ref[...] = summed.T * factor


def finish(parts, *terms):
    return pallas(
        finish_kernel,
        in_specs=[VMEM] * (1 + len(terms)),
        out_specs=[VMEM, VMEM],
        out_shape=[jax.ShapeDtypeStruct((128, 256), F32)] * 2,
        name="finish",
    )(parts, *terms)


def rotate_kernel(plane, where_ref, r_ref, *refs):
    chunk_refs, (out_ref, buf, turned, sems) = refs[:8], refs[-4:]

    for i in range(2):
        for d in range(8):
            start = 1024 * plane if d < WHOLE else 0
            source = chunk_refs[d].at[pl.ds(512 * i + start, 512)]
            target = buf.at[i, :, pl.ds(256 * d, 256)]
            pltpu.make_async_copy(source, target, sems.at[i, d]).start()

    @pl.loop(0, 8)
    def _(d):
        at = pl.multiple_of(where_ref[3 + d] * 256, 256)
        turned[pl.ds(pl.multiple_of(256 * d, 256), 256), :] = r_ref[pl.ds(at, 256), :]

    @pl.loop(0, 2)
    def _(i):
        for d in range(8):
            target = buf.at[i, :, pl.ds(256 * d, 256)]
            pltpu.make_async_copy(target, target, sems.at[i, d]).wait()
        rows = pl.ds(pl.multiple_of(512 * i, 512), 512)
        out_ref[0, rows, :] = nn(buf[i], turned[...]).astype(BF16)


def rotate(plane, where, r, pieces, *before):
    operands = [pieces[pieces_of(d)[plane if d >= WHOLE else 0][0]] for d in range(8)]
    return pallas(
        functools.partial(rotate_kernel, plane),
        grid=(1,),
        in_specs=[SMEM, VMEM] + [HBM] * 8 + [pl.BlockSpec(memory_space=pl.ANY)] * len(before),
        out_specs=pl.BlockSpec((1, 1024, 256), lambda i: (plane, 0, 0)),
        out_shape=jax.ShapeDtypeStruct((2, 1024, 256), BF16),
        scratch_shapes=[VM((2, 512, 2048), BF16), VM((2048, 256), BF16), DMA((2, 8))],
        input_output_aliases={10: 0} if before else {},
        name="rotate",
    )(where, r, *operands, *before)


def along_x(step):
    return [(x * 2 + y, ((x + step) % 4) * 2 + y) for x in range(4) for y in range(2)]


SWAP_Y = [(o, o ^ 1) for o in range(8)]
SWAP_CORE = [(g, g ^ 1) for g in range(16)]
SWAP_FAR = [(g, g ^ 2) for g in range(16)]


def along_z(step):
    return [(g, (g + 4 * step) % 16) for g in range(16)]


def exchange(blocks, groups=None):
    return lax.all_to_all(
        blocks, "grid", split_axis=0, concat_axis=0, tiled=True, axis_index_groups=groups
    )


def on_device(coefficients, potential, rotation):
    g = lax.axis_index("grid")
    o = lax.axis_index("orb")
    x, y = o // 2, o % 2
    xs = jnp.stack([x, x + 3, x + 1, x, x + 2, x + 3, x + 1, x + 2]) % 4
    ys = jnp.stack([y, y, y, 1 - y, y, 1 - y, 1 - y, 1 - y])
    place = jnp.stack([g // 4, (g // 2) % 2, g % 2])
    where = jnp.concatenate([place, xs * 2 + ys]).astype(jnp.int32)
    own = coefficients.reshape(2048, 256)
    behind = lax.ppermute(own, "orb", along_x(1))
    ahead = lax.ppermute(own, "orb", along_x(-1))
    blocks, rows, low, high = turn(coefficients.reshape(2, 1024, 256), potential)
    spread = exchange(blocks)
    side_low = lax.ppermute(low, "orb", SWAP_Y)
    side_high = lax.ppermute(high, "orb", SWAP_Y)
    far_low = lax.ppermute(behind[:1024], "orb", along_x(1))
    far_high = lax.ppermute(ahead[1024:], "orb", along_x(-1))
    behind_low = lax.ppermute(side_low, "orb", along_x(1))
    ahead_low = lax.ppermute(side_low, "orb", along_x(-1))
    behind_high = lax.ppermute(side_high, "orb", along_x(1))
    ahead_high = lax.ppermute(side_high, "orb", along_x(-1))
    last_low = lax.ppermute(far_low, "orb", SWAP_Y)
    last_high = lax.ppermute(far_high, "orb", SWAP_Y)
    pieces = [own, behind, ahead, side_low, side_high, far_low, far_high, behind_low, behind_high]
    pieces += [ahead_low, ahead_high, last_low, last_high]
    h = exchange(apply(spread))
    first = early(FIRST, rows, pieces)
    rotated = rotate(0, where, rotation, pieces)
    mine, theirs = inter(where, rows, first, pieces)
    other = lax.ppermute(theirs, "grid", SWAP_CORE)
    keep, give = pair(where, mine, other)
    got = lax.ppermute(give, "grid", SWAP_FAR)
    mine, theirs = proj(where, h, pieces)
    other = lax.ppermute(theirs, "grid", SWAP_CORE)
    groups = [[2 * i + c for i in range(8)] for c in range(2)]
    parts = exchange(plain(mine, other), groups)
    stays, *leaves = line(where, keep, got)
    terms = [stays] + [
        lax.ppermute(leaf, "grid", along_z(step))
        for step, leaf in zip((1, 2, 3), leaves)
    ]
    hamiltonian = unturn(h)
    rotated = rotate(1, where, rotation, pieces, rotated)
    projected, intersection = finish(parts, *terms)
    shape = coefficients.shape
    return (hamiltonian.reshape(shape), rotated.reshape(shape), projected, intersection)


def solution(mesh):
    placed = (P("grid", None, None, "orb"), P(None, "grid", None), P(None, "orb"))

    return jax.shard_map(
        on_device,
        mesh=mesh,
        in_specs=placed,
        out_specs=(
            P("grid", None, None, "orb"),
            P("grid", None, None, "orb"),
            P("grid", "orb"),
            P("grid", "orb"),
        ),
        check_vma=False,
    )
```

```python
import functools
import math

import jax
import jax.numpy as jnp
import numpy as np
from jax import lax
from jax.experimental import pallas as pl
from jax.experimental.pallas import tpu as pltpu
from jax.sharding import PartitionSpec as P

KC = 32
NG = 64
F32 = jnp.float32
BF16 = jnp.bfloat16
VM = pltpu.VMEM


def tables():
    points = np.arange(NG)
    modes = np.arange(KC) - KC // 2
    angles = ((points[:, None] * modes[None, :]) % NG).astype(np.float32) * np.float32(
        2.0 * math.pi / NG
    )
    waves = np.cos(angles) + np.sin(angles)
    forward = (waves / np.float32(math.sqrt(KC))).astype(BF16)
    backward = (waves.T / np.float32(math.sqrt(NG))).astype(BF16)
    return forward, backward


def operators():
    forward, backward = tables()
    eye8 = np.eye(8, dtype=np.float32)
    eye4 = np.eye(4, dtype=np.float32)
    fw = forward.astype(np.float32)
    bw = backward.astype(np.float32)
    w2 = np.einsum("xk,ij->kijx", fw, eye8).reshape(256, 512)
    t4 = np.einsum("kx,ij->kixj", bw, eye8).reshape(256, 512)
    w5 = np.einsum("kx,ij->kijx", bw, eye8).reshape(256, 512)
    t6 = np.einsum("kx,ij->ixjk", bw, eye4).reshape(256, 128)
    compact = np.tile(fw, (1, 8))
    compact = np.concatenate([compact[:32], compact[32:]], axis=1)
    t6 = np.concatenate([t6.T[:64], t6.T[64:]], axis=1)
    return jnp.asarray(np.concatenate([w2, t4, w5, t6, compact]).astype(BF16))


VMEM_LIMIT = 24 << 20


def pallas(kernel, limit=VMEM_LIMIT, **options):
    params = pltpu.CompilerParams(vmem_limit_bytes=limit)
    return pl.pallas_call(kernel, compiler_params=params, **options)


HBM = pl.BlockSpec(memory_space=pltpu.HBM)
VMEM = pl.BlockSpec(memory_space=VM)
SMEM = pl.BlockSpec(memory_space=pltpu.SMEM)


def nt(a, b):
    return lax.dot_general(a, b, (((1,), (1,)), ((), ())), preferred_element_type=F32)


def nn(a, b):
    return jnp.dot(a, b, preferred_element_type=F32)


def turn_kernel(c_ref, v_ref, blocks_ref, rows_ref):
    first = c_ref[0].astype(F32).T
    second = c_ref[1].astype(F32).T
    both = jnp.concatenate([first.reshape(16, 8, 1024), second.reshape(16, 8, 1024)], axis=1)
    blocks_ref[:, :32, :] = both.astype(BF16).reshape(8, 32, 1024)
    columns = [v_ref[:, j, :].T.reshape(4, 2, 8, NG) for j in range(4)]
    tiles = [jnp.concatenate([c[:, 0], c[:, 1]], axis=2) for c in columns]
    for p in range(4):
        for half in range(2):
            lanes = slice(256 * p + 128 * half, 256 * p + 128 * half + 128)
            tile = jnp.concatenate([tiles[2 * half][p], tiles[2 * half + 1][p]], axis=0)
            blocks_ref[:, 32:, lanes] = jnp.broadcast_to(tile.astype(BF16)[None], (8, 16, 128))
    rows_ref[:, :1024] = first.astype(BF16)
    rows_ref[:, 1024:] = second.astype(BF16)


def turn(c3, v):
    return pallas(
        turn_kernel,
        limit=None,
        grid=(2,),
        in_specs=[
            pl.BlockSpec((2, 1024, 128), lambda i: (0, 0, i)),
            pl.BlockSpec((NG, 4, NG), lambda i: (0, 0, 0)),
        ],
        out_specs=[
            pl.BlockSpec((8, 48, 1024), lambda i: (i, 0, 0)),
            pl.BlockSpec((128, 2048), lambda i: (i, 0)),
        ],
        out_shape=[
            pltpu.HBM((16, 48, 1024), BF16),
            pltpu.HBM((256, 2048), BF16),
        ],
        name="turn",
    )(c3, v)


def orbital_rows(h, plane):
    parts = h.astype(F32).reshape(-1, 16, 1024)[:, 8 * plane : 8 * plane + 8]
    return parts.reshape(-1, 1024)


def unturn_kernel(h_ref, out_ref):
    for plane in range(2):
        out_ref[plane] = orbital_rows(h_ref[...], plane).T.astype(BF16)


def unturn(h):
    return pallas(
        unturn_kernel,
        grid=(2,),
        in_specs=[pl.BlockSpec((8, 32, 1024), lambda i: (i, 0, 0))],
        out_specs=pl.BlockSpec((2, 1024, 128), lambda i: (0, 0, i)),
        out_shape=jax.ShapeDtypeStruct((2, 1024, 256), BF16),
        name="unturn",
    )(h)


def kinetic(lanes_from):
    k1 = lax.broadcasted_iota(jnp.int32, (256, 128), 0) // 8 - KC // 2
    at = lax.broadcasted_iota(jnp.int32, (256, 128), 1) + lanes_from
    k2, k3 = at // KC - KC // 2, at % KC - KC // 2
    return (k1 * k1 + k2 * k2 + k3 * k3).astype(F32) * (0.5 / (KC // 2) ** 2)


def apply_kernel(x_ref, v_ref, tables_ref, h_ref, t1_ref, t6_ref, y_ref, u_ref):
    w2_ref, t4_ref, w5_ref = [tables_ref.at[pl.ds(256 * i, 256)] for i in range(3)]

    @pl.when(pl.program_id(0) == 0)
    def _():
        shape = (32, 8, 256)
        same = lax.broadcasted_iota(jnp.int32, shape, 1) == (
            lax.broadcasted_iota(jnp.int32, shape, 2) // KC
        )
        for i in range(2):
            rows = tables_ref[832:, 256 * i : 256 * i + 256].astype(F32)
            spread = jnp.where(same, jnp.broadcast_to(rows[:, None, :], shape), 0.0)
            t1_ref[256 * i : 256 * i + 256] = spread.reshape(256, 256).astype(BF16)
        t6_ref[:64] = tables_ref[768:832, :256]
        t6_ref[64:] = tables_ref[768:832, 256:]

    for i in range(2):
        parts = [
            nt(t1_ref[...], x_ref[:, :, 256 * q : 256 * q + 256].reshape(256, 256))
            for q in (2 * i, 2 * i + 1)
        ]
        parts = [part.reshape(64, 8, 256) for part in parts]
        y_ref[:, 16 * i : 16 * i + 16, :] = jnp.concatenate(parts, axis=1).astype(BF16)
    low = lax.broadcasted_iota(jnp.int32, (512, 128), 1) < 64
    for p in range(4):
        v = jnp.concatenate(
            [v_ref[:, :, 256 * p + 128 * i : 256 * p + 128 * i + 128] for i in range(2)], axis=1
        )
        v = v.reshape(512, 128).astype(F32)
        swapped = pltpu.roll(v, 64, 1)
        tiles = (jnp.where(low, v, swapped), jnp.where(low, swapped, v))
        slabs = []
        both = nn(y_ref[16 * p : 16 * p + 16].reshape(512, 256), w2_ref[...]).astype(BF16)
        for i in range(2):
            real = nn(t1_ref[...], both[256 * i : 256 * i + 256])
            weighted = jnp.concatenate(
                [real[:, 128 * j : 128 * j + 128] * tiles[i] for j in range(4)], axis=1
            ).astype(BF16)
            slabs.append(nn(t4_ref[...], weighted).reshape(32, 8, 512))
        u_ref[:, 16 * p : 16 * p + 16, :] = jnp.concatenate(slabs, axis=1).astype(BF16)
    for q in range(8):
        u = u_ref[4 * q : 4 * q + 4].reshape(256, 512)
        back = nt(w5_ref[...], u).astype(BF16)
        h = nt(back, t6_ref[...])
        lanes = slice(128 * q, 128 * q + 128)
        h = h + kinetic(128 * q) * x_ref[:, :, lanes].reshape(256, 128).astype(F32)
        h_ref[:, :, lanes] = h.astype(BF16).reshape(16, 16, 128)


def apply(x):
    tables = operators()
    half = pl.BlockSpec((16, 16, 1024), lambda i: (0, i, 0))
    return pallas(
        apply_kernel,
        grid=(2,),
        in_specs=[half, pl.BlockSpec((16, 16, 1024), lambda i: (0, 2, 0))] + [VMEM],
        out_specs=half,
        scratch_shapes=[
            VM((512, 256), BF16),
            VM((128, 256), BF16),
            VM((64, 32, 256), BF16),
            VM((32, 64, 512), BF16),
        ],
        out_shape=pltpu.HBM((16, 32, 1024), BF16),
        name="apply",
    )(x, x, tables)


WHOLE = 3
PIECES = WHOLE + 2 * (8 - WHOLE)
DMA = pltpu.SemaphoreType.DMA


def pieces_of(d):
    if d < WHOLE:
        return [(d, 0, 2048)]
    at = WHOLE + 2 * (d - WHOLE)
    return [(at, 0, 1024), (at + 1, 1024, 1024)]


def used(chunks):
    return [piece for d in chunks for piece, _, _ in pieces_of(d)]


def fetch(refs, buf, sems, chunks):
    at = 0
    for slot, d in enumerate(chunks):
        parts = pieces_of(d)
        for half in range(2):
            if len(parts) == 1:
                source = refs[at].at[pl.ds(1024 * half, 1024)]
            else:
                source = refs[at + half]
            target = buf.at[slot, pl.ds(1024 * half, 1024)]
            pltpu.make_async_copy(source, target, sems.at[slot, half]).start()
        at += len(parts)


def product(lhs, buf, sems, slot):
    for half in range(2):
        target = buf.at[slot, pl.ds(1024 * half, 1024)]
        pltpu.make_async_copy(target, target, sems.at[slot, half]).wait()
    return nn(lhs[...], buf[slot]).astype(BF16)


FIRST = (0, 1, 2)
LATER = (3, 4, 7, 5, 6)


def early_kernel(chunks, rows_ref, *refs):
    chunk_refs, (out_ref, buf, rows, sems, sem) = refs[:-5], refs[-5:]
    load = pltpu.make_async_copy(rows_ref, rows, sem)
    load.start()
    fetch(chunk_refs, buf, sems, chunks)
    load.wait()

    @pl.loop(0, len(chunks))
    def _(slot):
        out_ref[slot] = product(rows, buf, sems, slot)


def early(chunks, rows, pieces):
    operands = [pieces[i] for i in used(chunks)]
    return pallas(
        functools.partial(early_kernel, chunks),
        in_specs=[HBM] * (1 + len(operands)),
        out_specs=VMEM,
        out_shape=pltpu.HBM((len(chunks), 256, 256), BF16),
        scratch_shapes=[
            VM((len(chunks), 2048, 256), BF16),
            VM((256, 2048), BF16),
            DMA((len(chunks), 2)),
            DMA,
        ],
        name="early",
    )(rows, *operands)


def put(where_ref, mine_ref, theirs_ref, d, value):
    block, even = where_ref[3 + d], where_ref[2] == 0
    mine_ref[block] = jnp.where(even, value[:, :128], value[:, 128:])
    theirs_ref[block] = jnp.where(even, value[:, 128:], value[:, :128])


SHARE = jax.ShapeDtypeStruct((8, 256, 128), BF16)


def inter_kernel(where_ref, rows_ref, first_ref, *refs):
    chunk_refs, (mine_ref, theirs_ref, buf, rows, done, sems, loads) = refs[:-7], refs[-7:]
    copies = [
        pltpu.make_async_copy(rows_ref, rows, loads.at[0]),
        pltpu.make_async_copy(first_ref, done, loads.at[1]),
    ]
    copies[0].start()
    fetch(chunk_refs, buf, sems, LATER)
    copies[1].start()
    copies[0].wait()

    @pl.loop(0, len(LATER))
    def _(slot):
        d = jnp.where(slot < 2, slot + 3, jnp.where(slot == 2, 7, slot + 2))
        put(where_ref, mine_ref, theirs_ref, d, product(rows, buf, sems, slot))

    copies[1].wait()
    for slot, d in enumerate(FIRST):
        put(where_ref, mine_ref, theirs_ref, d, done[slot])


def inter(where, rows, first, pieces):
    operands = [pieces[i] for i in used(LATER)]
    return pallas(
        inter_kernel,
        in_specs=[SMEM, HBM, HBM] + [HBM] * len(operands),
        out_specs=[VMEM, VMEM],
        out_shape=[SHARE, SHARE],
        scratch_shapes=[
            VM((len(LATER), 2048, 256), BF16),
            VM((256, 2048), BF16),
            VM((len(FIRST), 256, 256), BF16),
            DMA((len(LATER), 2)),
            DMA((2,)),
        ],
        name="inter",
    )(where, rows, first, *operands)


def proj_kernel(where_ref, h_ref, *refs):
    chunk_refs, (mine_ref, theirs_ref, buf, lhs, sems) = refs[:-5], refs[-5:]
    fetch(chunk_refs, buf, sems, range(8))
    for plane in range(2):
        lanes = slice(1024 * plane, 1024 * plane + 1024)
        lhs[:, lanes] = orbital_rows(h_ref[...], plane).astype(BF16)

    @pl.loop(0, 8)
    def _(d):
        put(where_ref, mine_ref, theirs_ref, d, product(lhs, buf, sems, d))


def proj(where, h, pieces):
    return pallas(
        proj_kernel,
        in_specs=[SMEM, VMEM] + [HBM] * PIECES,
        out_specs=[VMEM, VMEM],
        out_shape=[SHARE, SHARE],
        scratch_shapes=[
            VM((8, 2048, 256), BF16),
            VM((256, 2048), BF16),
            DMA((8, 2)),
        ],
        name="proj",
    )(where, h, *pieces)


BLOCKS4 = jax.ShapeDtypeStruct((4, 256, 128), BF16)
BLOCK = jax.ShapeDtypeStruct((256, 128), BF16)


def total(first, second):
    return (first.astype(F32) + second.astype(F32)).astype(BF16)


def pair_kernel(where_ref, mine_ref, other_ref, keep_ref, give_ref):
    far = where_ref[1]
    for z in range(4):
        keep, give = 2 * z + far, 2 * z + 1 - far
        keep_ref[z] = total(mine_ref[keep], other_ref[keep])
        give_ref[z] = total(mine_ref[give], other_ref[give])


def pair(where, mine, other):
    return pallas(
        pair_kernel,
        in_specs=[SMEM, VMEM, VMEM],
        out_specs=[VMEM, VMEM],
        out_shape=[BLOCKS4, BLOCKS4],
        name="pair",
    )(where, mine, other)


def line_kernel(where_ref, keep_ref, got_ref, *outs):
    for step, out in enumerate(outs):
        z = lax.rem(where_ref[0] + step, 4)
        out[...] = total(keep_ref[z], got_ref[z])


def line(where, keep, got):
    return pallas(
        line_kernel,
        in_specs=[SMEM, VMEM, VMEM],
        out_specs=[VMEM] * 4,
        out_shape=[pltpu.HBM(BLOCK.shape, BF16)] * 4,
        name="line",
    )(where, keep, got)


def plain_kernel(mine_ref, other_ref, total_ref):
    total_ref[...] = total(mine_ref[...], other_ref[...])


def plain(mine, other):
    block = pl.BlockSpec((4, 256, 128), lambda i: (i, 0, 0))
    return pallas(
        plain_kernel,
        grid=(2,),
        in_specs=[block, block],
        out_specs=block,
        out_shape=pltpu.HBM(SHARE.shape, BF16),
        name="plain",
    )(mine, other)


def finish_kernel(parts_ref, *refs):
    terms, (projected_ref, intersection_ref) = refs[:-2], refs[-2:]
    factor = 1.0 / float(KC * KC * KC)
    summed = parts_ref[0].astype(F32)
    for i in range(1, 8):
        summed = summed + parts_ref[i].astype(F32)
    projected_ref[...] = summed.T * factor
    summed = terms[0][...].astype(F32)
    for term in terms[1:]:
        summed = summed + term[...].astype(F32)
    intersection_ref[...] = summed.T * factor


def finish(parts, *terms):
    return pallas(
        finish_kernel,
        in_specs=[VMEM] * (1 + len(terms)),
        out_specs=[VMEM, VMEM],
        out_shape=[jax.ShapeDtypeStruct((128, 256), F32)] * 2,
        name="finish",
    )(parts, *terms)


def rotate_kernel(plane, where_ref, r_ref, *refs):
    chunk_refs, (out_ref, buf, sems) = refs[:8], refs[-3:]

    for i in range(2):
        for d in range(8):
            start = 1024 * plane if d < WHOLE else 0
            source = chunk_refs[d].at[pl.ds(512 * i + start, 512)]
            lanes = pl.ds(pl.multiple_of(where_ref[3 + d] * 256, 256), 256)
            pltpu.make_async_copy(source, buf.at[i, :, lanes], sems.at[i, d]).start()

    @pl.loop(0, 2)
    def _(i):
        for d in range(8):
            target = buf.at[i, :, pl.ds(256 * d, 256)]
            pltpu.make_async_copy(target, target, sems.at[i, d]).wait()
        rows = pl.ds(pl.multiple_of(512 * i, 512), 512)
        out_ref[0, rows, :] = nn(buf[i], r_ref[...]).astype(BF16)


def rotate(plane, where, r, pieces, *before):
    operands = [pieces[pieces_of(d)[plane if d >= WHOLE else 0][0]] for d in range(8)]
    return pallas(
        functools.partial(rotate_kernel, plane),
        grid=(1,),
        in_specs=[SMEM, VMEM] + [HBM] * 8 + [pl.BlockSpec(memory_space=pl.ANY)] * len(before),
        out_specs=pl.BlockSpec((1, 1024, 256), lambda i: (plane, 0, 0)),
        out_shape=jax.ShapeDtypeStruct((2, 1024, 256), BF16),
        scratch_shapes=[VM((2, 512, 2048), BF16), DMA((2, 8))],
        input_output_aliases={10: 0} if before else {},
        name="rotate",
    )(where, r, *operands, *before)


def along_x(step):
    return [(x * 2 + y, ((x + step) % 4) * 2 + y) for x in range(4) for y in range(2)]


SWAP_Y = [(o, o ^ 1) for o in range(8)]
SWAP_CORE = [(g, g ^ 1) for g in range(16)]
SWAP_FAR = [(g, g ^ 2) for g in range(16)]


def along_z(step):
    return [(g, (g + 4 * step) % 16) for g in range(16)]


def exchange(blocks, groups=None):
    return lax.all_to_all(
        blocks, "grid", split_axis=0, concat_axis=0, tiled=True, axis_index_groups=groups
    )


def on_device(coefficients, potential, rotation):
    g = lax.axis_index("grid")
    o = lax.axis_index("orb")
    x, y = o // 2, o % 2
    xs = jnp.stack([x, x + 3, x + 1, x, x + 2, x + 3, x + 1, x + 2]) % 4
    ys = jnp.stack([y, y, y, 1 - y, y, 1 - y, 1 - y, 1 - y])
    place = jnp.stack([g // 4, (g // 2) % 2, g % 2])
    where = jnp.concatenate([place, xs * 2 + ys]).astype(jnp.int32)
    own = coefficients.reshape(2048, 256)
    behind = lax.ppermute(own, "orb", along_x(1))
    ahead = lax.ppermute(own, "orb", along_x(-1))
    side_low = lax.ppermute(own[:1024], "orb", SWAP_Y)
    blocks, rows = turn(coefficients.reshape(2, 1024, 256), potential)
    spread = exchange(blocks)
    later, rows = lax.optimization_barrier((own, rows))
    side_high = lax.ppermute(later[1024:], "orb", SWAP_Y)
    far_low = lax.ppermute(behind[:1024], "orb", along_x(1))
    far_high = lax.ppermute(ahead[1024:], "orb", along_x(-1))
    behind_low = lax.ppermute(side_low, "orb", along_x(1))
    ahead_low = lax.ppermute(side_low, "orb", along_x(-1))
    behind_high = lax.ppermute(side_high, "orb", along_x(1))
    ahead_high = lax.ppermute(side_high, "orb", along_x(-1))
    last_low = lax.ppermute(far_low, "orb", SWAP_Y)
    last_high = lax.ppermute(far_high, "orb", SWAP_Y)
    pieces = [own, behind, ahead, side_low, side_high, far_low, far_high, behind_low, behind_high]
    pieces += [ahead_low, ahead_high, last_low, last_high]
    h = exchange(apply(spread))
    first = early(FIRST, rows, pieces)
    rotated = rotate(0, where, rotation, pieces)
    mine, theirs = inter(where, rows, first, pieces)
    other = lax.ppermute(theirs, "grid", SWAP_CORE)
    keep, give = pair(where, mine, other)
    got = lax.ppermute(give, "grid", SWAP_FAR)
    mine, theirs = proj(where, h, pieces)
    other = lax.ppermute(theirs, "grid", SWAP_CORE)
    groups = [[2 * i + c for i in range(8)] for c in range(2)]
    parts = exchange(plain(mine, other), groups)
    stays, *leaves = line(where, keep, got)
    terms = [stays] + [
        lax.ppermute(leaf, "grid", along_z(step))
        for step, leaf in zip((1, 2, 3), leaves)
    ]
    hamiltonian = unturn(h)
    rotated = rotate(1, where, rotation, pieces, rotated)
    projected, intersection = finish(parts, *terms)
    shape = coefficients.shape
    return (hamiltonian.reshape(shape), rotated.reshape(shape), projected, intersection)


def solution(mesh):
    placed = (P("grid", None, None, "orb"), P(None, "grid", None), P(None, "orb"))

    return jax.shard_map(
        on_device,
        mesh=mesh,
        in_specs=placed,
        out_specs=(
            P("grid", None, None, "orb"),
            P("grid", None, None, "orb"),
            P("grid", "orb"),
            P("grid", "orb"),
        ),
        check_vma=False,
    )
```
